256 devices in a mesh: front: 16 (over z, core), tile: 16 (over y, x).
Axes of the slice: x: 4, y: 4, z: 8, core: 2. Of those that a mesh axis runs over, the one named last changes fastest.
Arguments:
- pieces: bfloat16 [18432, 256, 128], P(('front', 'tile')), may hold values from -1.59375 to 1.59375
- dest_front: int32 [18432, 1], P(('front', 'tile')), may hold values from 0 to 15; in each aligned block of 72 rows (0 to 71, 72 to 143, ...) at most 9 rows name the same one
- dest_slot: int32 [18432], P(('front', 'tile')), may hold values from 0 to 3
- parent_u: bfloat16 [4096, 4096], P('front', 'tile'), may hold values from -1.59375 to 1.59375
- parent_v: bfloat16 [4096, 4096], P('front', 'tile'), may hold values from -1.59375 to 1.59375
- sketch: bfloat16 [256, 64], replicated, may hold values from -6 to 6
- pivot_inverse: bfloat16 [4096, 256], P('front'), may hold values from -0.01171875 to 0.01171875
Outputs:
- coeff: bfloat16 [4096, 4096], P('front', 'tile')
- cores: float32 [65536, 4096], P(('front', 'tile'))
The draws below stay inside these ranges and needn't reach their ends.
Inputs may be any that keep to these rules, and one draw needn't show every extreme that they name: `dest_front`: among the 72 rows of one device at most 9 name any one front, a bound that some block reaches.
All inputs are finite; a program needn't handle non-finite values.
Results may differ from the reference program's by a relative error of at most 0.017.
Values may be sent and summed in bfloat16 or wider, within the bound.
No kernel may reach another device: no remote copies, remote signals or barrier semaphores. Data moves between devices by JAX's collectives and lax.ppermute only.
A program may use at most 128 MiB of HBM per device.

```python
import math
import jax
import jax.numpy as jnp
import numpy as np
from jax import lax

B = 256
R = 64
TILES_DEV = 4
PIECES = 72
CAP = 9
TILES = 64
N_FRONT = 16
N_TILE = 16


def set_ends(drawn, key, smallest, high):
    longest = drawn.shape.index(max(drawn.shape))
    spots = []
    for shift in (0, 1):
        where = [jax.random.randint(jax.random.fold_in(key, axis), (), 0, length) for axis, length in enumerate(drawn.shape)]
        where[longest] = (where[longest] + shift) % drawn.shape[longest]
        spots.append(tuple(where))
    return drawn.at[spots[0]].set(smallest).at[spots[1]].set(high)


def block_scale(key, extent, cuts, low, largest):
    loudness, own = 1.0, jax.random.fold_in(key, 6)
    for dim, blocks in cuts:
        heights = jnp.exp(jax.random.uniform(jax.random.fold_in(own, dim), (blocks,), jnp.float32, low / len(cuts), largest / len(cuts)))
        loudness = loudness * jnp.repeat(heights, extent[dim] // blocks).reshape([-1 if axis == dim else 1 for axis in range(len(extent))])
    return loudness


def deal_out(rng, own, number, rows, count, top, reach, lean):
    order = jax.random.permutation(rng, count)
    heavy_load, common = shares(count, rows * top, reach, lean, True), shares(count, rows * top, reach, lean, False)
    places = jnp.arange(count)

    def named(sizes, rotation):
        used = int((sizes > 0).sum())
        fixed = max(1, used // 4)
        shifted = fixed + (places - fixed + rotation * (used - fixed)) % max(1, count - fixed)
        return jnp.zeros((count,), jnp.int32).at[order[jnp.where(places < fixed, places, shifted)]].set(jnp.asarray(sizes, jnp.int32))

    sizes = jnp.where(number % 4 == 0, named(heavy_load, number // 4), named(common, number - number // 4 - 1))
    mixed = jax.random.permutation(jax.random.fold_in(own, 3), count)
    donor, sink = mixed[0:count // 2 * 2:2], mixed[1:count // 2 * 2:2]
    margin = jnp.minimum(sizes[donor] - 1, reach - sizes[sink]) // 2
    margin = jnp.where((donor == order[0]) | (sink == order[0]) | (sizes[sink] == 0), 0, jnp.maximum(margin, 0))
    shifted = jax.random.randint(jax.random.fold_in(own, 4), (count // 2,), 0, 1 << 20) % (margin + 1)
    sizes = sizes.at[donor].add(-shifted).at[sink].add(shifted)
    members = jnp.searchsorted(jnp.cumsum(sizes), jnp.arange(rows * top), side="right").astype(jnp.int32)
    listing = members.reshape(top, rows).T
    listing = listing[jax.random.permutation(jax.random.fold_in(own, 1), rows)]
    rotation = jax.random.randint(jax.random.fold_in(own, 2), (rows, 1), 0, top)
    return jnp.take_along_axis(listing, (jnp.arange(top)[None, :] + rotation) % top, axis=1)


def shares(number_of, total, reach, slope, full):
    weights = [(1 << 20) // math.isqrt(grade ** slope) + 1 for grade in range(1, number_of + 1)]
    largest = reach if full else min(reach, max(-(-total // number_of), total * weights[0] // sum(weights)))
    least = 1 if total - largest >= number_of - 1 else 0
    counts, rest = [largest] + [least] * (number_of - 1), total - largest - least * (number_of - 1)
    while rest > 0:
        candidates = [i for i in range(1, number_of) if counts[i] < largest] or [i for i in range(1, number_of) if counts[i] < reach]
        mass, budget = sum([weights[i] for i in candidates]), rest
        for i in candidates:
            more = min(reach - counts[i], max(1, budget * weights[i] // mass), rest)
            counts[i] = counts[i] + more
            rest = rest - more
    return np.array(counts)


def gaussian(rng, dims, deviation, bound, cuts=(), kind=jnp.bfloat16):
    values = jax.random.normal(rng, dims, jnp.float32) * deviation
    if len(cuts) > 0:
        values = block_scale(rng, dims, cuts, -0.22, 0.18) * values
    return jnp.clip(values, min=-bound, max=bound).astype(kind)


def setup_inputs(seed: int = 0) -> dict:
    key_of = jax.random.split(jax.random.key(seed), 8)
    pieces = gaussian(key_of[0], (N_FRONT * N_TILE * PIECES, B, 2 * R), 0.2, 1.59375, ((0, 256),))
    dest_front_keys = jax.random.split(jax.random.fold_in(key_of[1], 1), (N_FRONT * N_TILE * PIECES) // PIECES)
    dest_front_turns = jax.random.permutation(jax.random.fold_in(key_of[1], 3), (N_FRONT * N_TILE * PIECES) // PIECES)
    dest_front = jax.vmap(lambda own, number: deal_out(jax.random.fold_in(key_of[1], 2), own, number, PIECES, N_FRONT, 1, CAP, 2))(dest_front_keys, dest_front_turns).reshape((N_FRONT * N_TILE * PIECES, 1))
    dest_slot = set_ends(jax.random.randint(key_of[2], (N_FRONT * N_TILE * PIECES,), 0, TILES_DEV), jax.random.fold_in(key_of[2], 1), 0, TILES_DEV - 1).astype(jnp.int32)
    parent_u = gaussian(key_of[3], (N_FRONT * B, TILES * R), 0.2, 1.59375, ((0, 16), (1, 16)))
    parent_v = gaussian(key_of[4], (N_FRONT * B, TILES * R), 0.2, 1.59375, ((0, 16), (1, 16)))
    sketch = gaussian(key_of[5], (B, R), 1.0, 6.0)
    pivot_inverse = gaussian(key_of[6], (N_FRONT * B, B), (4 * B * B) ** -0.5, 0.01171875, ((0, 16),))
    return {"pieces": pieces, "dest_front": dest_front, "dest_slot": dest_slot, "parent_u": parent_u, "parent_v": parent_v, "sketch": sketch, "pivot_inverse": pivot_inverse}


def rounded(field_values):
    return lax.optimization_barrier(field_values.astype(jnp.bfloat16)).astype(jnp.float32)

def orthonormal_basis(block_unit):
    gram_matrix = jnp.einsum('naj,nav->njv', block_unit, block_unit, precision=lax.Precision.HIGHEST)
    lower = jnp.linalg.cholesky(gram_matrix)
    solved = jax.scipy.linalg.solve_triangular(lower, jnp.swapaxes(block_unit, 1, 2), lower=True)
    return jnp.swapaxes(solved, 1, 2)

def reference(pieces, dest_front, dest_slot, parent_u, parent_v, sketch, pivot_inverse):
    tile_total = N_TILE * TILES_DEV
    tile_count = N_FRONT * tile_total
    row_ids = jnp.arange(N_FRONT * N_TILE * PIECES, dtype=jnp.int32)
    source_tile = row_ids // PIECES % N_TILE
    target_block = (dest_front[:, 0] * tile_total + source_tile * TILES_DEV + dest_slot).astype(jnp.int32)
    blocks = pieces.reshape(N_FRONT * N_TILE, PIECES, B, 2 * R)
    targets = target_block.reshape(N_FRONT * N_TILE, PIECES)

    def tile_major(field_values):
        return field_values.reshape(N_FRONT, B, tile_total, R).transpose(0, 2, 1, 3).reshape(tile_count, B, R).astype(jnp.float32)

    def front_major(field_values):
        return field_values.reshape(N_FRONT, tile_total, B, R).transpose(0, 2, 1, 3).reshape(N_FRONT * B, tile_total * R)
    owned_left_rows = tile_major(parent_u)
    own_right = tile_major(parent_v)
    sketch_full = sketch.astype(jnp.float32)

    def accumulate(term):

        def advance(running, block_unit):
            group, where = block_unit
            left_rows = group[..., :R].astype(jnp.float32)
            right_rows = group[..., R:].astype(jnp.float32)
            return (running + jax.ops.segment_sum(term(left_rows, right_rows, where), where, num_segments=tile_count), None)
        summed, unused = lax.scan(advance, jnp.zeros((tile_count, B, R), jnp.float32), (blocks, targets))
        return summed

    def expand(factor, small):
        return jnp.einsum('pbr,prk->pbk', factor, small)

    def project(factor, other):
        return rounded(jnp.einsum('pbr,pbk->prk', factor, other))

    def sketch_term(left_rows, right_rows, where):
        return expand(left_rows, rounded(jnp.einsum('pbr,bk->prk', right_rows, sketch_full)))
    y_start = accumulate(sketch_term) + sketch_term(owned_left_rows, own_right, None)
    q_start = rounded(orthonormal_basis(y_start))

    def back_term(left_rows, right_rows, where):
        return expand(right_rows, project(left_rows, q_start[where]))
    tile_ids = jnp.arange(tile_count, dtype=jnp.int32)
    z_mid = rounded(accumulate(back_term) + back_term(owned_left_rows, own_right, tile_ids))

    def forth_term(left_rows, right_rows, where):
        return expand(left_rows, project(right_rows, z_mid[where]))
    y_end = accumulate(forth_term) + forth_term(owned_left_rows, own_right, tile_ids)
    q_end = rounded(orthonormal_basis(y_end))

    def final_term(left_rows, right_rows, where):
        return expand(right_rows, project(left_rows, q_end[where]))
    w_end = accumulate(final_term) + final_term(owned_left_rows, own_right, tile_ids)
    coeff = front_major(w_end).astype(jnp.bfloat16)

    def couple(front_pair):
        block_unit, inverse = front_pair
        pivoted = jnp.dot(inverse.astype(jnp.float32), block_unit.astype(jnp.float32), preferred_element_type=jnp.float32).astype(jnp.bfloat16)
        return jnp.dot(block_unit.T.astype(jnp.float32), pivoted.astype(jnp.float32), preferred_element_type=jnp.float32)
    stacked = lax.map(couple, (coeff.reshape(N_FRONT, B, tile_total * R), pivot_inverse.reshape(N_FRONT, B, B)))
    cores = stacked.reshape(N_FRONT * tile_total * R, tile_total * R)
    return (coeff, cores)
```

```python
import jax
import jax.numpy as jnp
from jax import lax
from jax.experimental import pallas as pl
from jax.experimental.pallas import tpu as pltpu
from jax.sharding import PartitionSpec as P

B = 256
R = 64
TILES_DEV = 4
PIECES = 72
CAP = 9
FRONTS = 16
RING = 8
ROW = 4
BF = jnp.bfloat16
F32 = jnp.float32
HIGHEST = lax.Precision.HIGHEST
TILE = (TILES_DEV, B, B)
VM = pltpu.VMEM


def nt_dot(a, b, precision=None):
    return lax.dot_general(
        a, b, (((1,), (1,)), ((), ())), precision=precision, preferred_element_type=F32
    )


def densify_kernel(distances, front_ref, slot_ref, me_ref, pieces_ref, *rest):
    outs = rest[: 2 * len(distances)]
    table, count, zero = rest[2 * len(distances) :]

    @pl.loop(0, FRONTS * TILES_DEV)
    def _(g):
        count[g] = 0

    @pl.loop(0, PIECES)
    def _(p):
        g = front_ref[p] * TILES_DEV + slot_ref[p]
        n = count[g]
        table[g * CAP + n] = p
        count[g] = n + 1

    zero[...] = jnp.zeros_like(zero)
    low = lax.broadcasted_iota(jnp.int32, (B, 2 * R), 1) < R

    def swapped(x):
        return jnp.concatenate([x[:, R:], x[:, :R]], axis=1)

    def quad(g, base, have):
        got = []
        for j in range(4):
            index = jnp.where(base + j < have, table[g * CAP + jnp.minimum(base + j, CAP - 1)], PIECES)
            index = jnp.where(base + j < have, index, 0)
            x = pieces_ref[index]
            got.append(jnp.where(base + j < have, x, jnp.zeros_like(x)))
        turned = [swapped(x) for x in got]
        left = jnp.concatenate(
            [jnp.where(low, got[0], turned[1]), jnp.where(low, got[2], turned[3])], axis=1
        )
        right = jnp.concatenate(
            [jnp.where(low, turned[0], got[1]), jnp.where(low, turned[2], got[3])], axis=1
        )
        return nt_dot(left, right)

    for i, distance in enumerate(distances):
        for side in range(2):
            out = outs[2 * i + side]
            z = lax.rem(me_ref[0] + distance, RING)
            core = me_ref[1] if side == 1 else 1 - me_ref[1]
            front = 2 * z + core

            for slot in range(TILES_DEV):
                g = front * TILES_DEV + slot
                have = count[g]
                out[slot] = quad(g, 0, have).astype(BF)

                @pl.when(have > 4)
                def _(g=g, have=have, out=out, slot=slot):
                    more = quad(g, 4, have) + quad(g, 8, have)
                    out[slot] = (quad(g, 0, have) + more).astype(BF)


def densify(front, slot, me, pieces, distances):
    whole = pl.BlockSpec((PIECES, B, 2 * R), lambda i, *_: (0, 0, 0), pipeline_mode=pl.Buffered(1))
    result = pl.BlockSpec(TILE, lambda i, *_: (0, 0, 0), pipeline_mode=pl.Buffered(1))
    count = 2 * len(distances)
    return pl.pallas_call(
        lambda *refs: densify_kernel(distances, *refs),
        grid_spec=pltpu.PrefetchScalarGridSpec(
            num_scalar_prefetch=3,
            grid=(1,),
            in_specs=[whole],
            out_specs=[result] * count,
            scratch_shapes=[
                pltpu.SMEM((FRONTS * TILES_DEV * CAP,), jnp.int32),
                pltpu.SMEM((FRONTS * TILES_DEV,), jnp.int32),
                VM((8, 128), F32),
            ],
        ),
        out_shape=[jax.ShapeDtypeStruct(TILE, BF)] * count,
        cost_estimate=pl.CostEstimate(
            flops=count * 4 * 2 * B**3, bytes_accessed=count * B * B * 8, transcendentals=0
        ),
        name=f"densify{len(distances)}",
    )(front, slot, me, pieces)


def inverse_factors(grams):
    eye = (
        lax.broadcasted_iota(jnp.int32, (R, R), 0) == lax.broadcasted_iota(jnp.int32, (R, R), 1)
    ).astype(F32)
    rows = [jnp.concatenate([g, eye], axis=1) for g in grams]
    rows = [[a[8 * b : 8 * b + 8] for b in range(R // 8)] for a in rows]
    sub = lax.broadcasted_iota(jnp.int32, (8, 2 * R), 0)
    for k in range(R - 1):
        b, r = k // 8, k % 8
        for a in rows:
            row = jnp.broadcast_to(a[b][r : r + 1], (8, 2 * R))
            pivot = jnp.broadcast_to(row[:, k : k + 1], (8, 2 * R))
            row = row * (1.0 / pivot)
            for c in range(b, R // 8):
                factor = jnp.broadcast_to(a[c][:, k : k + 1], (8, 2 * R))
                if c == b:
                    factor = jnp.where(sub > r, factor, 0.0)
                a[c] = a[c] - factor * row
    result = []
    for a in rows:
        full = jnp.concatenate(a, axis=0)
        diagonal = jnp.sum(full[:, :R] * eye, axis=1, keepdims=True)
        result.append(full[:, R:] * lax.rsqrt(diagonal))
    return result


def bases(ys):
    inverses = inverse_factors([nt_dot(y, y, HIGHEST) for y in ys])
    return [
        jnp.dot(inverse, y, precision=HIGHEST, preferred_element_type=F32).astype(BF)
        for inverse, y in zip(inverses, ys)
    ]


def recompress_kernel(
    own, got, low_up, low_down, high_up, high_down, pu, pv, sketch_t, pinv, wt_ref, coeff_ref, piv_ref
):
    tiles, turned = [], []
    for t in range(TILES_DEV):
        up, down = (low_up, low_down) if t < 2 else (high_up, high_down)
        m = own[t].astype(F32) + got[t].astype(F32) + up[t % 2].astype(F32) + down[t % 2].astype(F32)
        cols = slice(t * R, (t + 1) * R)
        m = m + nt_dot(pu[:, cols], pv[:, cols])
        tiles.append(m.astype(BF))
        turned.append(m.T.astype(BF))

    def times(small, dense):
        return jnp.dot(small, dense, preferred_element_type=F32)

    q = bases([times(sketch_t[...], x) for x in turned])
    z = [times(a, m).astype(BF) for a, m in zip(q, tiles)]
    q = bases([times(a, x) for a, x in zip(z, turned)])
    w = jnp.concatenate([times(a, m) for a, m in zip(q, tiles)], axis=0)
    wt_ref[...] = w.astype(BF)
    coeff = w.T.astype(BF)
    coeff_ref[...] = coeff
    piv_ref[...] = times(pinv[...], coeff).astype(BF)


def recompress(*operands):
    block = jax.ShapeDtypeStruct((B, TILES_DEV * R), BF)
    return pl.pallas_call(
        recompress_kernel,
        in_specs=[pl.BlockSpec(memory_space=VM)] * len(operands),
        out_specs=[pl.BlockSpec(memory_space=VM)] * 3,
        out_shape=[block] * 3,
        name="recompress",
    )(*operands)


def couple_kernel(place_ref, wt_ref, block_ref, *rest):
    out_ref = rest[-1]
    out_ref[...] = jnp.dot(wt_ref[...], block_ref[0], preferred_element_type=F32)


def couple(place, wt, blocks, cores=None):
    n = blocks.shape[0]
    shape = jax.ShapeDtypeStruct((B, ROW * ROW * B), F32)
    in_specs = [
        pl.BlockSpec((B, B), lambda i, place: (0, 0)),
        pl.BlockSpec((1, B, B), lambda i, place: (i, 0, 0)),
    ]
    operands = [place, wt, blocks]
    if cores is not None:
        in_specs.append(pl.BlockSpec(memory_space=pl.ANY))
        operands.append(cores)
    return pl.pallas_call(
        couple_kernel,
        grid_spec=pltpu.PrefetchScalarGridSpec(
            num_scalar_prefetch=1,
            grid=(n,),
            in_specs=in_specs,
            out_specs=pl.BlockSpec((B, B), lambda i, place: (0, place[i])),
        ),
        out_shape=shape,
        input_output_aliases={} if cores is None else {3: 0},
        cost_estimate=pl.CostEstimate(
            flops=2 * n * B**3, bytes_accessed=n * B * B * 6, transcendentals=0
        ),
        name=f"couple{n}",
    )(*operands)


def shards(pieces, dest_front, dest_slot, parent_u, parent_v, sketch, pivot_inverse):
    here = lax.axis_index("front")
    me = jnp.stack([here // 2, here % 2]).astype(jnp.int32)
    tile = lax.axis_index("tile")
    swap = [(i, i ^ 1) for i in range(FRONTS)]
    up = [(i, (i + 2) % FRONTS) for i in range(FRONTS)]
    down = [(i, (i - 2) % FRONTS) for i in range(FRONTS)]

    own, got = {}, {}
    for distances in ((4,), (3, 5), (2, 6, 1, 7, 0)):
        parts = densify(dest_front[:, 0], dest_slot, me, pieces, distances)
        for i, d in enumerate(distances):
            got[d] = lax.ppermute(parts[2 * i], "front", swap)
            own[d] = parts[2 * i + 1]

    low, high = slice(0, 2), slice(2, 4)

    def total(d, part, *more):
        s = own[d][part].astype(F32) + got[d][part].astype(F32)
        for x in more:
            s = s + x.astype(F32)
        return s.astype(BF)

    low_up = lax.ppermute(total(4, low), "front", up)
    high_down = lax.ppermute(total(4, high), "front", down)
    high_up = lax.ppermute(total(3, high), "front", up)
    low_down = lax.ppermute(total(5, low), "front", down)
    low_up = lax.ppermute(total(3, low, low_up), "front", up)
    high_down = lax.ppermute(total(5, high, high_down), "front", down)
    for d in (2, 1):
        high_up = lax.ppermute(total(d, high, high_up), "front", up)
        low_down = lax.ppermute(total(8 - d, low, low_down), "front", down)
        low_up = lax.ppermute(total(d, low, low_up), "front", up)
        high_down = lax.ppermute(total(8 - d, high, high_down), "front", down)

    wt, coeff, pivoted = recompress(
        own[0], got[0], low_up, low_down, high_up, high_down,
        parent_u, parent_v, sketch.T, pivot_inverse,
    )

    along_x = lambda k: [(y * ROW + x, y * ROW + (x + k) % ROW) for y in range(ROW) for x in range(ROW)]
    along_y = lambda k: [(y * ROW + x, (y + k) % ROW * ROW + x) for y in range(ROW) for x in range(ROW)]
    send = lambda v, pairs: lax.ppermute(v, "tile", pairs)
    left = send(pivoted, along_x(1))
    right = send(pivoted, along_x(-1))
    far = jnp.concatenate(
        [send(left[: B // 2], along_x(1)), send(right[B // 2 :], along_x(-1))], axis=0
    )
    row = jnp.stack([pivoted, left, right, far])
    above = send(row, along_y(1))
    below = send(row, along_y(-1))
    apart = [send(above[:2], along_y(1)), send(below[2:], along_y(-1))]

    y, x = tile // ROW, tile % ROW
    xs = jnp.stack([x, (x + 3) % ROW, (x + 1) % ROW, (x + 2) % ROW]).astype(jnp.int32)
    at = lambda k: (y + k) % ROW * ROW + xs
    cores = couple(at(0), wt, row)
    cores = couple(at(3), wt, above, cores)
    cores = couple(at(1), wt, below, cores)
    cores = couple(at(2)[:2], wt, apart[0], cores)
    cores = couple(at(2)[2:], wt, apart[1], cores)
    return (coeff, cores)


def solution(mesh):
    return jax.shard_map(
        shards,
        mesh=mesh,
        in_specs=(
            P(("front", "tile"), None, None),
            P(("front", "tile"), None),
            P(("front", "tile")),
            P("front", "tile"),
            P("front", "tile"),
            P(),
            P("front", None),
        ),
        out_specs=(P("front", "tile"), P(("front", "tile"), None)),
        check_vma=False,
    )
```
